256 devices in a mesh: replica: 8 (over z_lo, y), tensor: 32 (over x, z_hi, core).
Axes of the slice: x: 4, y: 4, z: 8 (z_hi: 4, z_lo: 2; z = z_hi * 2 + z_lo), core: 2. Of those that a mesh axis runs over, the one named last changes fastest.
Arguments:
- activations: bfloat16 [65536, 832], P(('replica', 'tensor')), may hold values from -6 to 6
- out_grad: bfloat16 [65536, 14336], P('replica', 'tensor'), may hold values from -0.0625 to 0.0625
- master_weights: float32 [6656, 14336], P('replica', 'tensor'), may hold values from -6 to 6
- first_moment: float32 [6656, 14336], P('replica', 'tensor'), may hold values from -0.6 to 0.6
- second_moment: float32 [6656, 14336], P('replica', 'tensor'), may hold values from 0.01 to 1
- anchor: float32 [832, 14336], P(None, 'tensor'), may hold values from -6 to 6
- outer_momentum: float32 [832, 14336], P(None, 'tensor'), may hold values from -3 to 3
Outputs:
- rebuilt_weights: bfloat16 [832, 14336], P(None, 'tensor')
- new_momentum: float32 [832, 14336], P(None, 'tensor')
The draws below stay inside these ranges and needn't reach their ends.
All inputs are finite; a program needn't handle non-finite values.
Results may differ from the reference program's by a relative error of at most 0.001.
Values may be sent and summed in bfloat16 or wider, within the bound.
A program may use at most 128 MiB of HBM per device.

```python
import math
import jax
import jax.numpy as jnp
from jax import lax

FRAG = 832
TOK_DEV = 256
FF = 14336
GROUP_TOK = 8192
ALL_TOK = 65536
ALL_ROWS = 6656
N_REPLICA = 8
N_TENSOR = 32


def steps_of(rng, dims, shards, least, largest):
    loudness = 1.0
    for axis_at, parts in shards:
        steps = jax.random.uniform(jax.random.fold_in(jax.random.fold_in(rng, 6), axis_at), (parts,), jnp.float32, least / len(shards), largest / len(shards))
        loudness = loudness * jnp.repeat(jnp.exp(steps), dims[axis_at] // parts).reshape((-1,) + (1,) * (len(dims) - 1 - axis_at))
    return loudness


def normal_values(stream_key, shape, width, limit, cuts=(), kind=jnp.bfloat16):
    values = width * jax.random.normal(stream_key, shape, jnp.float32)
    if cuts:
        values = values * steps_of(stream_key, shape, cuts, -0.22, 0.18)
    return jnp.clip(values, -limit, limit).astype(kind)


def setup_inputs(seed: int = 0) -> dict:
    arg_keys = jax.random.split(jax.random.key(seed), 8)
    activations = normal_values(arg_keys[0], (ALL_TOK, FRAG), 1.0, 6.0, ((0, 256),))
    out_grad = normal_values(arg_keys[1], (ALL_TOK, FF), GROUP_TOK ** -0.5, 0.0625, ((0, 8), (1, 32)))
    master_weights = normal_values(arg_keys[2], (ALL_ROWS, FF), 1.0, 6.0, ((0, 8), (1, 32)), jnp.float32)
    first_moment = normal_values(arg_keys[3], (ALL_ROWS, FF), 0.1, 0.6, ((0, 8), (1, 32)), jnp.float32)
    second_moment = jnp.clip(jnp.exp(math.log(1.0) - 4.6051702 * jax.random.uniform(arg_keys[4], (ALL_ROWS, FF), jnp.float32) ** steps_of(arg_keys[4], (ALL_ROWS, FF), ((0, 8), (1, 32)), -0.2, 0.2)), 0.01, 1.0)
    anchor = normal_values(arg_keys[5], (FRAG, FF), 1.0, 6.0, ((1, 32),), jnp.float32)
    outer_momentum = normal_values(arg_keys[6], (FRAG, FF), 0.5, 3.0, ((1, 32),), jnp.float32)
    return dict(activations=activations, out_grad=out_grad, master_weights=master_weights, first_moment=first_moment, second_moment=second_moment, anchor=anchor, outer_momentum=outer_momentum)


BETA_ONE = 0.9
BETA_TWO = 0.95
BIAS_ONE = 0.9999734386
BIAS_TWO = 0.9940794708
EPSILON = 1e-08
INNER_RATE = 0.25
DECAY_RATE = 0.1
OUTER_RATE = 0.7
NESTEROV = 0.9

def reference(activations, out_grad, master_weights, first_moment, second_moment, anchor, outer_momentum):
    group_rows = TOK_DEV * N_TENSOR
    summed = jnp.zeros(anchor.shape, jnp.float32)
    for replica_id in range(N_REPLICA):
        block_acts = activations[replica_id * group_rows:(replica_id + 1) * group_rows]
        block_grad = out_grad[replica_id * group_rows:(replica_id + 1) * group_rows]
        gradient = lax.dot_general(block_acts, block_grad, (((0,), (0,)), ((), ())), preferred_element_type=jnp.float32)
        lower = replica_id * FRAG
        weights = master_weights[lower:lower + FRAG]
        moment_one = BETA_ONE * first_moment[lower:lower + FRAG] + (1.0 - BETA_ONE) * gradient
        moment_two = BETA_TWO * second_moment[lower:lower + FRAG] + (1.0 - BETA_TWO) * gradient * gradient
        step_size = moment_one / BIAS_ONE / (jnp.sqrt(moment_two / BIAS_TWO) + EPSILON)
        updated = weights - INNER_RATE * (step_size + DECAY_RATE * weights)
        summed = summed + (anchor - updated)
    pseudo_mean = summed / N_REPLICA
    new_momentum = NESTEROV * outer_momentum + pseudo_mean
    rebuilt = anchor - OUTER_RATE * (pseudo_mean + NESTEROV * new_momentum)
    return (rebuilt.astype(jnp.bfloat16), new_momentum)
```

```python
import heapq

import jax
import jax.numpy as jnp
from jax import lax
from jax.experimental import pallas as pl
from jax.experimental.pallas import tpu as pltpu
from jax.sharding import PartitionSpec as P

BETA_ONE = 0.9
BETA_TWO = 0.95
BIAS_ONE = 0.9999734386
BIAS_TWO = 0.9940794708
EPSILON = 1e-08
INNER_RATE = 0.25
DECAY_RATE = 0.1
OUTER_RATE = 0.7
NESTEROV = 0.9

MESH = pl.DeviceIdType.MESH
NX, NZ, NC = 4, 4, 2
RING = (0, -1, 1, 2)

SIZES = (384, 256, 192)
RATE = {"x": 45e3, "z": 22e3, "d": 200e3}
DELAY = {"x": 2.0, "z": 3.0, "d": 1.0}
MATMUL_US, UPDATE_US, EXCHANGE_US = 15.0, 4.0, 26.0


def transfers(p):
    moves = {
        ("zA", p, 1): ("z", (0, 0), "all", 1, (0, -1)),
        ("zA", p, -1): ("z", (0, 0), "all", -1, (0, 1)),
        ("zB", p, 1): ("z", (0, -1), "low", 1, (0, -2)),
        ("zB", p, -1): ("z", (0, 1), "high", -1, (0, 2)),
    }
    for dz in RING:
        moves["xA", p, 1, dz] = ("x", (0, dz), "all", 1, (-1, dz))
        moves["xA", p, -1, dz] = ("x", (0, dz), "all", -1, (1, dz))
        moves["xB", p, 1, dz] = ("x", (-1, dz), "low", 1, (-2, dz))
        moves["xB", p, -1, dz] = ("x", (1, dz), "high", -1, (2, dz))
        for dx in RING:
            moves["D", p, dx, dz] = ("d", (dx, dz), "all", 0, (dx, dz))
    return moves


def plan(sizes):
    phases = len(sizes)
    total = sum(sizes)
    moves = {}
    for p in range(phases):
        moves.update(transfers(p))
    rules = []

    def own_z(p):
        return [("zA", p, 1), ("zA", p, -1)] if p < phases else []

    def own_x(p):
        return [("xA", p, 1, 0), ("xA", p, -1, 0)] if p < phases else []

    for p in range(phases):
        rules.append(([("zA", p, 1)], [("zB", p, 1), ("xA", p, 1, -1), ("xA", p, -1, -1), ("D", p, 0, -1)]))
        rules.append(([("zA", p, -1)], [("zB", p, -1), ("xA", p, 1, 1), ("xA", p, -1, 1), ("D", p, 0, 1)] + own_z(p + 1) + own_x(p + 2)))
        rules.append(([("zB", p, 1), ("zB", p, -1)], [("xA", p, 1, 2), ("xA", p, -1, 2), ("D", p, 0, 2)]))
        for dz in RING:
            rules.append(([("xA", p, 1, dz)], [("xB", p, 1, dz), ("D", p, -1, dz)]))
            rules.append(([("xA", p, -1, dz)], [("xB", p, -1, dz), ("D", p, 1, dz)]))
            rules.append(([("xB", p, 1, dz), ("xB", p, -1, dz)], [("D", p, 2, dz)]))
    steps, arrivals, free, done = [], [], {}, set()
    clock = 0.0
    serial = 0

    def send(names):
        nonlocal serial
        for name in names:
            link, _, part, way, _ = moves[name]
            lane = (link, way)
            size = sizes[name[1]] * 512 * (1.0 if part == "all" else 0.5)
            begin = max(clock, free.get(lane, 0.0))
            free[lane] = begin + size / RATE[link]
            heapq.heappush(arrivals, (free[lane] + DELAY[link], serial, name))
            serial += 1
        steps.append(("send", tuple(names)))

    def exchange(name, p):
        nonlocal serial
        begin = max(clock, free.get("y", 0.0))
        free["y"] = begin + EXCHANGE_US * sizes[p] / total
        heapq.heappush(arrivals, (free["y"] + 3.0, serial, (name, p)))
        serial += 1

    send(own_z(0) + own_x(0))
    send([("D", p, 0, 0) for p in range(phases)])
    send(own_x(1))
    arrived = set()
    tasks = []
    for p in range(phases):
        for dx in RING:
            needs = {("D", p, dx, dz) for dz in RING}
            for dz in RING:
                for name, move in moves.items():
                    if name[0] != "D" and name[1] == p and move[4] in ((dx, dz), (dx - 4, dz), (dx, dz - 4)):
                        needs.add(name)
            tasks.append((("mm", p, dx), needs, MATMUL_US / 4 * sizes[p] / total))
        tasks.append((("update", p), {("mm", p, dx) for dx in RING}, UPDATE_US * sizes[p] / total))
        tasks.append((("reduce", p), {("RS", p)}, UPDATE_US / 8 * sizes[p] / total))
        tasks.append((("final", p), {("AG", p)}, UPDATE_US / 2 * sizes[p] / total))
    waited = set()
    while rules or tasks:
        while arrivals and arrivals[0][0] <= clock:
            arrived.add(heapq.heappop(arrivals)[2])
        rule = next((r for r in rules if set(r[0]) <= arrived), None)
        if rule:
            rules.remove(rule)
            for name in rule[0]:
                waited.add(name)
                steps.append(("wait", name))
            send(rule[1])
            continue
        ready = [t for t in tasks if t[1] <= (arrived | done)]
        if ready:
            rank = {"final": 3, "reduce": 0, "update": 1, "mm": 2}
            task = min(ready, key=lambda t: rank[t[0][0]])
            tasks.remove(task)
            for name in sorted(task[1] - waited - done, key=str):
                waited.add(name)
                steps.append(("wait", name))
            steps.append(task[0])
            clock += task[2]
            done.add(task[0])
            if task[0][0] == "update":
                exchange("RS", task[0][1])
            if task[0][0] == "reduce":
                exchange("AG", task[0][1])
            continue
        clock = arrivals[0][0]
    return steps, moves, clock


def make_kernel(sizes, features, hidden, tokens, replicas):
    steps, moves, _ = plan(sizes)
    starts = [sum(sizes[:p]) for p in range(len(sizes))]
    index = {name: i for i, name in enumerate(sorted(moves, key=str))}
    share = hidden // replicas

    def kernel(
        act, grad, w_hbm, m_hbm, v_hbm, an_hbm, mo_hbm, reb_ref, mom_ref,
        held, g_buf, w_buf, m_buf, v_buf, an_buf, mo_buf, acc, landed, mean,
        out_sem, in_sem, rs_out, rs_in, ag_out, ag_in, load_sem,
    ):
        me_r, me_t = lax.axis_index("replica"), lax.axis_index("tensor")
        core = lax.rem(me_t, NC)
        zh = lax.rem(me_t // NC, NZ)
        x = me_t // (NC * NZ)

        def slot(dx, dz, c):
            return (lax.rem(x + dx + NX, NX) * NZ + lax.rem(zh + dz + NZ, NZ)) * NC + c

        def device(dx, dz, c):
            return {"replica": me_r, "tensor": slot(dx, dz, c)}

        def peer(j):
            return lax.rem(me_r + j + replicas, replicas)

        loads = [
            pltpu.make_async_copy(src, dst, load_sem.at[i])
            for i, (src, dst) in enumerate(
                ((act, held.at[me_t]), (grad, g_buf), (w_hbm, w_buf), (m_hbm, m_buf), (v_hbm, v_buf), (an_hbm, an_buf), (mo_hbm, mo_buf))
            )
        ]
        for load in loads:
            load.start()

        barrier = pltpu.get_barrier_semaphore()
        friends = [device(0, 1, core), device(0, -1, core), device(1, 0, core), device(-1, 0, core), device(0, 0, 1 - core)]
        friends += [{"replica": peer(j), "tensor": me_t} for j in range(1, replicas)]
        for friend in friends:
            pl.semaphore_signal(barrier, inc=1, device_id=friend, device_id_type=MESH)
        pl.semaphore_wait(barrier, len(friends))

        def rows_of(name):
            p, part = name[1], moves[name][2]
            half = sizes[p] // 2
            begin = starts[p] + (half if part == "high" else 0)
            return pl.ds(begin, sizes[p] if part == "all" else half)

        def outgoing(name):
            link, source, _, way, _ = moves[name]
            rows = rows_of(name)
            there = slot(*source, core)
            target = {"x": device(way, 0, core), "z": device(0, way, core), "d": device(0, 0, 1 - core)}[link]
            src = act.at[rows] if source == (0, 0) else held.at[there, rows]
            return pltpu.make_async_remote_copy(
                src_ref=src,
                dst_ref=held.at[there, rows],
                send_sem=out_sem.at[index[name]],
                recv_sem=in_sem.at[index[name]],
                device_id=target,
                device_id_type=MESH,
            )

        def incoming(name):
            link, _, _, _, got = moves[name]
            place = held.at[slot(*got, 1 - core if link == "d" else core), rows_of(name)]
            return pltpu.make_async_remote_copy(
                src_ref=place,
                dst_ref=place,
                send_sem=out_sem.at[index[name]],
                recv_sem=in_sem.at[index[name]],
                device_id=device(0, 0, 1 - core),
                device_id_type=MESH,
            )

        def columns(p):
            return pl.ds(starts[p], sizes[p])

        def share_rows(r):
            return pl.ds(pl.multiple_of(r * share, 8), share)

        def scatter(p, j):
            return pltpu.make_async_remote_copy(
                src_ref=acc.at[share_rows(peer(j)), columns(p)],
                dst_ref=landed.at[j - 1, :, columns(p)],
                send_sem=rs_out.at[p, j - 1],
                recv_sem=rs_in.at[p, j - 1],
                device_id={"replica": peer(j), "tensor": me_t},
                device_id_type=MESH,
            )

        def spread(p, j, owner):
            return pltpu.make_async_remote_copy(
                src_ref=mean.at[share_rows(owner), columns(p)],
                dst_ref=mean.at[share_rows(owner), columns(p)],
                send_sem=ag_out.at[p, j - 1],
                recv_sem=ag_in.at[p, j - 1],
                device_id={"replica": peer(j), "tensor": me_t},
                device_id_type=MESH,
            )

        def matmul(p, dx, first):
            base = lax.rem(x + dx + NX, NX) * (NZ * NC)
            cols = columns(p)

            def product(i):
                block = base + i
                left = g_buf[:, pl.ds(pl.multiple_of(block * tokens, tokens), tokens)]
                return lax.dot_general(left, held[block, cols, :], (((1,), (1,)), ((), ())), preferred_element_type=jnp.float32)

            if first:
                acc[:, cols] = product(0) + product(1)

            @pl.loop(1 if first else 0, NZ * NC // 2)
            def _(i):
                acc[:, cols] += product(2 * i) + product(2 * i + 1)

        def update(p):
            cols = columns(p)
            step = 32

            @pl.loop(0, hidden // step)
            def _(i):
                rows = pl.ds(pl.multiple_of(i * step, step), step)
                gradient = acc[rows, cols]
                weights = w_buf[rows, cols]
                moment_one = BETA_ONE * m_buf[rows, cols] + (1.0 - BETA_ONE) * gradient
                moment_two = BETA_TWO * v_buf[rows, cols] + (1.0 - BETA_TWO) * gradient * gradient
                size = moment_one * (1.0 / BIAS_ONE) / (jnp.sqrt(moment_two * (1.0 / BIAS_TWO)) + EPSILON)
                updated = weights - INNER_RATE * (size + DECAY_RATE * weights)
                acc[rows, cols] = an_buf[rows, cols] - updated

        def reduce(p):
            cols = columns(p)
            rows = share_rows(me_r)
            total = acc[rows, cols]
            for j in range(1, replicas):
                total = total + landed[j - 1, :, cols]
            mean[rows, cols] = total * (1.0 / replicas)

        def final(p):
            cols = columns(p)
            step = 32

            @pl.loop(0, hidden // step)
            def _(i):
                rows = pl.ds(pl.multiple_of(i * step, step), step)
                pseudo_mean = mean[rows, cols]
                new_momentum = NESTEROV * mo_buf[rows, cols] + pseudo_mean
                mom_ref[rows, cols] = new_momentum
                rebuilt = an_buf[rows, cols] - OUTER_RATE * (pseudo_mean + NESTEROV * new_momentum)
                reb_ref[rows, cols] = rebuilt.astype(reb_ref.dtype)

        multiplied, loaded = set(), set()

        def load_wait(*which):
            for i in which:
                if i not in loaded:
                    loaded.add(i)
                    loads[i].wait()

        for kind, *rest in steps:
            if kind == "send":
                for name in rest[0]:
                    outgoing(name).start()
            elif kind == "wait":
                name = rest[0]
                if name[0] == "RS":
                    for j in range(1, replicas):
                        scatter(name[1], j).wait_recv()
                elif name[0] == "AG":
                    for j in range(1, replicas):
                        spread(name[1], j, peer(-j)).wait_recv()
                else:
                    incoming(name).wait_recv()
            elif kind == "mm":
                load_wait(0, 1)
                p, dx = rest
                matmul(p, dx, p not in multiplied)
                multiplied.add(p)
            elif kind == "update":
                load_wait(2, 3, 4, 5)
                update(rest[0])
                for j in range(1, replicas):
                    scatter(rest[0], j).start()
            elif kind == "reduce":
                reduce(rest[0])
                for j in range(1, replicas):
                    spread(rest[0], j, me_r).start()
            elif kind == "final":
                load_wait(6)
                final(rest[0])
        for name in index:
            outgoing(name).wait_send()
        for p in range(len(sizes)):
            for j in range(1, replicas):
                scatter(p, j).wait_send()
                spread(p, j, me_r).wait_send()

    count = len(index)
    full = (hidden, features)
    scratch = [
        pltpu.VMEM((NX * NZ * NC, features, tokens), jnp.bfloat16),
        pltpu.VMEM((hidden, NX * NZ * NC * tokens), jnp.bfloat16),
        *[pltpu.VMEM(full, jnp.float32)] * 5,
        pltpu.VMEM(full, jnp.float32),
        pltpu.VMEM((replicas - 1, share, features), jnp.float32),
        pltpu.VMEM(full, jnp.float32),
        pltpu.SemaphoreType.DMA((count,)),
        pltpu.SemaphoreType.DMA((count,)),
        *[pltpu.SemaphoreType.DMA((len(sizes), replicas - 1))] * 4,
        pltpu.SemaphoreType.DMA((7,)),
    ]
    return kernel, scratch


def on_device(activations, out_grad, master_weights, first_moment, second_moment, anchor, outer_momentum):
    tokens, features = activations.shape
    hidden = out_grad.shape[1]
    replicas = lax.axis_size("replica")
    kernel, scratch = make_kernel(SIZES, features, hidden, tokens, replicas)
    rebuilt, momentum = pl.pallas_call(
        kernel,
        out_shape=(
            jax.ShapeDtypeStruct((hidden, features), jnp.bfloat16),
            jax.ShapeDtypeStruct((hidden, features), jnp.float32),
        ),
        in_specs=[pl.BlockSpec(memory_space=pl.ANY)] * 7,
        out_specs=(pl.BlockSpec(memory_space=pltpu.VMEM),) * 2,
        scratch_shapes=scratch,
        compiler_params=pltpu.CompilerParams(collective_id=0, has_side_effects=True, vmem_limit_bytes=60 * 2**20),
        name="diloco",
    )(*(a.T for a in (activations, out_grad, master_weights, first_moment, second_moment, anchor, outer_momentum)))
    return rebuilt.T, momentum.T


def solution(mesh):
    placed = (
        P(("replica", "tensor"), None),
        P("replica", "tensor"),
        P("replica", "tensor"),
        P("replica", "tensor"),
        P("replica", "tensor"),
        P(None, "tensor"),
        P(None, "tensor"),
    )
    return jax.shard_map(
        on_device,
        mesh=mesh,
        in_specs=placed,
        out_specs=(P(None, "tensor"), P(None, "tensor")),
        check_vma=False,
    )
```

```python
import heapq

import jax
import jax.numpy as jnp
from jax import lax
from jax.experimental import pallas as pl
from jax.experimental.pallas import tpu as pltpu
from jax.sharding import PartitionSpec as P

BETA_ONE = 0.9
BETA_TWO = 0.95
BIAS_ONE = 0.9999734386
BIAS_TWO = 0.9940794708
EPSILON = 1e-08
INNER_RATE = 0.25
DECAY_RATE = 0.1
OUTER_RATE = 0.7
NESTEROV = 0.9

MESH = pl.DeviceIdType.MESH
NX, NZ, NC = 4, 4, 2
RING = (0, -1, 1, 2)

PHASES = ((256, "z"), (128, "x"), (256, "z"), (128, "z"), (64, "z"))
DIRECT = (4,)
RATE = {"x": 44e3, "z": 22e3, "d": 300e3, "y": 75e3}
DELAY = {"x": 2.0, "z": 2.7, "d": 1.0, "y": 2.5}
LEAD, BACKLOG = 1, 1.0
TILE_US, UPDATE_US, SEND_US = 3.5, 4.0, 0.02
OTHER = {"x": "z", "z": "x"}


def offset(first, a, b):
    return (a, b) if first == "x" else (b, a)


def transfers(p, first):
    second = OTHER[first]
    moves = {
        (1, p, 1): (first, (0, 0), "all", 1, offset(first, -1, 0)),
        (1, p, -1): (first, (0, 0), "all", -1, offset(first, 1, 0)),
        (2, p, 1): (first, offset(first, -1, 0), "low", 1, offset(first, 2, 0)),
        (2, p, -1): (first, offset(first, 1, 0), "high", -1, offset(first, 2, 0)),
    }
    for a in RING:
        moves[3, p, 1, a] = (second, offset(first, a, 0), "all", 1, offset(first, a, -1))
        moves[3, p, -1, a] = (second, offset(first, a, 0), "all", -1, offset(first, a, 1))
        moves[4, p, 1, a] = (second, offset(first, a, -1), "low", 1, offset(first, a, 2))
        moves[4, p, -1, a] = (second, offset(first, a, 1), "high", -1, offset(first, a, 2))
        for b in RING:
            moves[(5, p, *offset(first, a, b))] = ("d", offset(first, a, b), "all", 0, offset(first, a, b))
    return moves


GROUPS = ((0, -1), (1, 2))


def plan(phases, hidden):
    total = sum(f for f, _ in phases)
    moves, rules, tasks = {}, [], []
    for p, (_, first) in enumerate(phases):
        moves.update(transfers(p, first))
        third = lambda a: [(3, p, 1, a), (3, p, -1, a)]
        follow = lambda a, b: (5, p, *offset(first, a, b))
        rules.append(([(1, p, 1)], [(2, p, 1)] + third(-1) + [follow(-1, 0)]))
        rules.append(([(1, p, -1)], [(2, p, -1)] + third(1) + [follow(1, 0)]))
        rules.append(([(2, p, 1), (2, p, -1)], third(2) + [follow(2, 0)]))
        for a in RING:
            rules.append(([(3, p, 1, a)], [(4, p, 1, a), follow(a, -1)]))
            rules.append(([(3, p, -1, a)], [(4, p, -1, a), follow(a, 1)]))
            rules.append(([(4, p, 1, a), (4, p, -1, a)], [follow(a, 2)]))
        size = phases[p][0]
        needs_all = set()
        for dx in RING:
            for group in GROUPS:
                needs = {n for n, m in moves.items() if n[1] == p and m[4][0] == dx and m[4][1] in group}
                tasks.append((("mm", p, dx, group), needs, TILE_US / 8 * -(-size // 256)))
                needs_all.add(("mm", p, dx, group))
        share = UPDATE_US * size / total
        tasks.append((("update", p), needs_all, share))
        if p in DIRECT:
            tasks.append((("reduce", p), {("RS", p)}, share / 8))
        else:
            tasks.append((("halve", p), {("RS", p)}, share / 8))
            tasks.append((("reduce", p), {("PAIR", p)}, share / 16))
            tasks.append((("forward", p), {("AGZ", p)}, 0.02))
        tasks.append((("final", p), {("AG", p)}, share / 2))

    steps, arrivals, free, done, arrived, waited = [], [], {}, set(), set(), set()
    pending = {}
    clock, serial = 0.0, 0

    def urgency(name):
        stage, p = name[:2]
        return p - LEAD * (stage < 3) - 0.25 * (stage in (2, 4)), stage != 3 or name[3] != 2

    def request(names):
        for name in names:
            link, _, _, way, _ = moves[name]
            pending.setdefault((link, way), []).append(name)

    def push(name, lane, took, delay):
        nonlocal serial
        free[lane] = max(clock, free.get(lane, 0.0)) + took
        heapq.heappush(arrivals, (free[lane] + delay, serial, name))
        serial += 1

    def pump():
        nonlocal clock
        sent = []
        for lane, names in pending.items():
            while names and free.get(lane, 0.0) - clock < BACKLOG:
                name = min(names, key=urgency)
                names.remove(name)
                size = phases[name[1]][0] * 512 * (1.0 if moves[name][2] == "all" else 0.5)
                push(name, lane, size / RATE[lane[0]], DELAY[lane[0]])
                clock += SEND_US
                sent.append(name)
        if sent:
            steps.append(("send", tuple(sent)))

    def exchange(kind, p):
        size = phases[p][0] * hidden * 4
        if kind == "RS" or kind == "AG" and p in DIRECT:
            push((kind, p), "y", size * 0.75 / RATE["y"], DELAY["y"] + (p in DIRECT))
        elif kind == "forward":
            push(("AG", p), "y", size * 0.375 / RATE["y"], DELAY["y"])
        elif kind == "PAIR":
            push((kind, p), ("z", 1), size / 8 / RATE["x"], DELAY["x"])
        else:
            push(("AGY", p), "y", size * 0.375 / RATE["y"], DELAY["y"])
            push(("AGZ", p), ("z", 1), size / 8 / RATE["x"], DELAY["x"])

    for p, (_, first) in enumerate(phases):
        request([(1, p, 1), (1, p, -1), (3, p, 1, 0), (3, p, -1, 0), (5, p, 0, 0)])
    pump()
    rank = {"reduce": 0, "halve": 1, "forward": 2, "update": 3, "mm": 4, "final": 5}
    after = {"update": "RS", "halve": "PAIR", "reduce": "AG", "forward": "forward"}
    while rules or tasks:
        while arrivals and arrivals[0][0] <= clock:
            arrived.add(heapq.heappop(arrivals)[2])
        rule = next((r for r in rules if set(r[0]) <= arrived), None)
        if rule:
            rules.remove(rule)
            for name in rule[0]:
                waited.add(name)
                steps.append(("wait", name))
            request(rule[1])
            pump()
            continue
        ready = [t for t in tasks if t[1] <= (arrived | done)]
        if ready:
            task = min(ready, key=lambda t: (rank[t[0][0]], t[0][1]))
            tasks.remove(task)
            for name in sorted(task[1] - waited - done, key=str):
                waited.add(name)
                steps.append(("wait", name))
            steps.append(task[0])
            clock += task[2]
            done.add(task[0])
            if task[0][0] in after:
                exchange(after[task[0][0]], task[0][1])
            pump()
            continue
        clock = arrivals[0][0]
        pump()
    return steps, moves, clock


def make_kernel(phases, features, hidden, tokens, replicas):
    steps, moves, _ = plan(phases, hidden)
    sizes = [f for f, _ in phases]
    starts = [sum(sizes[:p]) for p in range(len(sizes))]
    index = {name: i for i, name in enumerate(sorted(moves, key=str))}
    share = hidden // replicas
    ny = replicas // 2

    def kernel(
        act, grad, w_hbm, m_hbm, v_hbm, an_hbm, mo_hbm, reb_ref, mom_ref,
        held, g_buf, w_buf, m_buf, v_buf, an_buf, mo_buf, acc, landed, mean,
        out_sem, in_sem, rs_out, rs_in, ag_out, ag_in, load_sem,
    ):
        me_r, me_t = lax.axis_index("replica"), lax.axis_index("tensor")
        core = lax.rem(me_t, NC)
        zh = lax.rem(me_t // NC, NZ)
        x = me_t // (NC * NZ)
        zl = me_r // ny
        y = lax.rem(me_r, ny)

        def slot(dx, dz, c):
            return (lax.rem(x + dx + NX, NX) * NZ + lax.rem(zh + dz + NZ, NZ)) * NC + c

        def device(dx, dz, c):
            return {"replica": me_r, "tensor": slot(dx, dz, c)}

        def place(j, sign=1):
            there = lax.rem(zl + j // ny, 2)
            return there, lax.rem(y + sign * (j % ny) + ny, ny)

        def replica(j):
            there, row = place(j)
            return {"replica": there * ny + row, "tensor": me_t}

        loads = [
            pltpu.make_async_copy(src, dst, load_sem.at[i])
            for i, (src, dst) in enumerate(
                ((act, held.at[me_t]), (grad, g_buf), (w_hbm, w_buf), (m_hbm, m_buf), (v_hbm, v_buf), (an_hbm, an_buf), (mo_hbm, mo_buf))
            )
        ]
        for load in loads:
            load.start()

        barrier = pltpu.get_barrier_semaphore()
        friends = [device(0, 1, core), device(0, -1, core), device(1, 0, core), device(-1, 0, core), device(0, 0, 1 - core)]
        friends += [replica(j) for j in range(1, replicas)]
        for friend in friends:
            pl.semaphore_signal(barrier, inc=1, device_id=friend, device_id_type=MESH)
        pl.semaphore_wait(barrier, len(friends))

        def rows_of(name):
            p, part = name[1], moves[name][2]
            half = sizes[p] // 2
            begin = starts[p] + (half if part == "high" else 0)
            return pl.ds(begin, sizes[p] if part == "all" else half)

        def outgoing(name):
            link, source, _, way, _ = moves[name]
            rows = rows_of(name)
            there = slot(*source, core)
            target = {"x": device(way, 0, core), "z": device(0, way, core), "d": device(0, 0, 1 - core)}[link]
            src = act.at[rows] if source == (0, 0) else held.at[there, rows]
            return pltpu.make_async_remote_copy(
                src_ref=src,
                dst_ref=held.at[there, rows],
                send_sem=out_sem.at[index[name]],
                recv_sem=in_sem.at[index[name]],
                device_id=target,
                device_id_type=MESH,
            )

        def incoming(name):
            link, _, _, _, got = moves[name]
            spot = held.at[slot(*got, 1 - core if link == "d" else core), rows_of(name)]
            return pltpu.make_async_remote_copy(
                src_ref=spot,
                dst_ref=spot,
                send_sem=out_sem.at[index[name]],
                recv_sem=in_sem.at[index[name]],
                device_id=device(0, 0, 1 - core),
                device_id_type=MESH,
            )

        def columns(p):
            return pl.ds(starts[p], sizes[p])

        def shares(place, count=1):
            there, row = place
            return pl.ds(pl.multiple_of(row * 2 * share + (there * share if count == 1 else 0), 8), count * share)

        def remote(src, dst, out, into, target):
            return pltpu.make_async_remote_copy(
                src_ref=src, dst_ref=dst, send_sem=out, recv_sem=into, device_id=target, device_id_type=MESH
            )

        def scatter(p):
            cols = columns(p)
            if p in DIRECT:
                for j in range(1, replicas):
                    at = j - 1
                    dst = landed.at[pl.ds(at * share, share), cols]
                    yield remote(acc.at[shares(place(j)), cols], dst, rs_out.at[p, at], rs_in.at[p, at], replica(j))
            else:
                for j in range(1, ny):
                    at = j - 1
                    dst = landed.at[pl.ds(at * 2 * share, 2 * share), cols]
                    yield remote(acc.at[shares(place(j), 2), cols], dst, rs_out.at[p, at], rs_in.at[p, at], replica(j))

        def pair(p):
            cols, at = columns(p), ny - 1
            dst = landed.at[pl.ds(at * 2 * share, share), cols]
            return remote(acc.at[shares(place(ny)), cols], dst, rs_out.at[p, at], rs_in.at[p, at], replica(ny))

        def spread(p, sent=True, offsets=None):
            cols = columns(p)
            for j in offsets or range(1, replicas if p in DIRECT else ny + 1):
                ref = mean.at[shares((zl, y) if sent else place(j, -1)), cols]
                yield remote(ref, ref, ag_out.at[p, j - 1], ag_in.at[p, j - 1], replica(j))

        def forward(p, sent=True):
            cols = columns(p)
            for j in range(1, ny):
                there, row = place(j, -1)
                ref = mean.at[shares((1 - zl, y) if sent else (1 - zl, row)), cols]
                yield remote(ref, ref, ag_out.at[p, ny + j - 1], ag_in.at[p, ny + j - 1], replica(j))

        def matmul(p, dx, group, first):
            cols = columns(p)

            def product(dz, c):
                block = slot(dx, dz, c)
                left = g_buf[:, pl.ds(pl.multiple_of(block * tokens, tokens), tokens)]
                return lax.dot_general(left, held[block, cols, :], (((1,), (1,)), ((), ())), preferred_element_type=jnp.float32)

            low = min(group)
            if first:
                acc[:, cols] = product(low, 0) + product(low, 1)

            @pl.loop(1 if first else 0, len(group))
            def _(i):
                acc[:, cols] += product(low + i, 0) + product(low + i, 1)

        def update(p):
            cols = columns(p)
            step = 32

            @pl.loop(0, hidden // step)
            def _(i):
                rows = pl.ds(pl.multiple_of(i * step, step), step)
                gradient = acc[rows, cols]
                weights = w_buf[rows, cols]
                moment_one = BETA_ONE * m_buf[rows, cols] + (1.0 - BETA_ONE) * gradient
                moment_two = BETA_TWO * v_buf[rows, cols] + (1.0 - BETA_TWO) * gradient * gradient
                size = moment_one * (1.0 / BIAS_ONE) / (jnp.sqrt(moment_two * (1.0 / BIAS_TWO)) + EPSILON)
                updated = weights - INNER_RATE * (size + DECAY_RATE * weights)
                acc[rows, cols] = an_buf[rows, cols] - updated

        def halve(p):
            cols = columns(p)
            for there in (1 - zl, zl):
                rows = shares((there, y))
                total = acc[rows, cols]
                for j in range(ny - 1):
                    total = total + landed[pl.ds(pl.multiple_of(j * 2 * share + there * share, 8), share), cols]
                acc[rows, cols] = total

        def reduce(p):
            cols = columns(p)
            rows = shares((zl, y))
            total = acc[rows, cols]
            for at in range(replicas - 1) if p in DIRECT else (replicas - 2,):
                total = total + landed[pl.ds(at * share, share), cols]
            mean[rows, cols] = total * (1.0 / replicas)

        def final(p):
            cols = columns(p)
            step = 32

            @pl.loop(0, hidden // step)
            def _(i):
                rows = pl.ds(pl.multiple_of(i * step, step), step)
                pseudo_mean = mean[rows, cols]
                new_momentum = NESTEROV * mo_buf[rows, cols] + pseudo_mean
                mom_ref[rows, cols] = new_momentum
                rebuilt = an_buf[rows, cols] - OUTER_RATE * (pseudo_mean + NESTEROV * new_momentum)
                reb_ref[rows, cols] = rebuilt.astype(reb_ref.dtype)

        multiplied, loaded = set(), set()

        def load_wait(*which):
            for i in which:
                if i not in loaded:
                    loaded.add(i)
                    loads[i].wait()

        def wait(name):
            kind, p = name[:2]
            if kind == "RS":
                for copy in scatter(p):
                    copy.wait_recv()
            elif kind == "PAIR":
                pair(p).wait_recv()
            elif kind == "AGZ":
                for copy in spread(p, False, (ny,)):
                    copy.wait_recv()
            elif kind == "AG":
                for copy in spread(p, False, range(1, replicas if p in DIRECT else ny)):
                    copy.wait_recv()
                if p not in DIRECT:
                    for copy in forward(p, False):
                        copy.wait_recv()
            else:
                incoming(name).wait_recv()

        for kind, *rest in steps:
            p = rest[0]
            if kind == "send":
                for name in rest[0]:
                    outgoing(name).start()
            elif kind == "forward":
                for copy in forward(p):
                    copy.start()
            elif kind == "wait":
                wait(rest[0])
            elif kind == "mm":
                load_wait(0, 1)
                matmul(*rest, p not in multiplied)
                multiplied.add(p)
            elif kind == "update":
                load_wait(2, 3, 4, 5)
                update(p)
                for copy in scatter(p):
                    copy.start()
            elif kind == "halve":
                halve(p)
                pair(p).start()
            elif kind == "reduce":
                reduce(p)
                for copy in spread(p):
                    copy.start()
            elif kind == "final":
                load_wait(6)
                final(p)
        for name in index:
            outgoing(name).wait_send()
        for p in range(len(sizes)):
            copies = [*scatter(p), *spread(p)]
            if p not in DIRECT:
                copies += [pair(p), *forward(p)]
            for copy in copies:
                copy.wait_send()

    count = len(index)
    full = (hidden, features)
    scratch = [
        pltpu.VMEM((NX * NZ * NC, features, tokens), jnp.bfloat16),
        pltpu.VMEM((hidden, NX * NZ * NC * tokens), jnp.bfloat16),
        *[pltpu.VMEM(full, jnp.float32)] * 5,
        pltpu.VMEM(full, jnp.float32),
        pltpu.VMEM(((replicas - 1) * share, features), jnp.float32),
        pltpu.VMEM(full, jnp.float32),
        pltpu.SemaphoreType.DMA((count,)),
        pltpu.SemaphoreType.DMA((count,)),
        *[pltpu.SemaphoreType.DMA((len(sizes), replicas - 1))] * 4,
        pltpu.SemaphoreType.DMA((7,)),
    ]
    return kernel, scratch


def on_device(activations, out_grad, master_weights, first_moment, second_moment, anchor, outer_momentum):
    tokens, features = activations.shape
    hidden = out_grad.shape[1]
    replicas = lax.axis_size("replica")
    kernel, scratch = make_kernel(PHASES, features, hidden, tokens, replicas)
    rebuilt, momentum = pl.pallas_call(
        kernel,
        out_shape=(
            jax.ShapeDtypeStruct((hidden, features), jnp.bfloat16),
            jax.ShapeDtypeStruct((hidden, features), jnp.float32),
        ),
        in_specs=[pl.BlockSpec(memory_space=pl.ANY)] * 7,
        out_specs=(pl.BlockSpec(memory_space=pltpu.VMEM),) * 2,
        scratch_shapes=scratch,
        compiler_params=pltpu.CompilerParams(collective_id=0, has_side_effects=True, vmem_limit_bytes=60 * 2**20),
        name="diloco",
    )(*(a.T for a in (activations, out_grad, master_weights, first_moment, second_moment, anchor, outer_momentum)))
    return rebuilt.T, momentum.T


def solution(mesh):
    placed = (
        P(("replica", "tensor"), None),
        P("replica", "tensor"),
        P("replica", "tensor"),
        P("replica", "tensor"),
        P("replica", "tensor"),
        P(None, "tensor"),
        P(None, "tensor"),
    )
    return jax.shard_map(
        on_device,
        mesh=mesh,
        in_specs=placed,
        out_specs=(P(None, "tensor"), P(None, "tensor")),
        check_vma=False,
    )
```

```python
import heapq

import jax
import jax.numpy as jnp
from jax import lax
from jax.experimental import pallas as pl
from jax.experimental.pallas import tpu as pltpu
from jax.sharding import PartitionSpec as P

BETA_ONE = 0.9
BETA_TWO = 0.95
BIAS_ONE = 0.9999734386
BIAS_TWO = 0.9940794708
EPSILON = 1e-08
INNER_RATE = 0.25
DECAY_RATE = 0.1
OUTER_RATE = 0.7
NESTEROV = 0.9

MESH = pl.DeviceIdType.MESH
NX, NZ, NC = 4, 4, 2
RING = (0, -1, 1, 2)

PHASES = ((256, "z"), (128, "x"), (256, "z"), (128, "z"), (64, "z"))
MODES = ("yz", "yz", "yz", "yz", "all")
RATE = {"x": 44e3, "z": 22e3, "d": 300e3, "y": 75e3}
DELAY = {"x": 2.0, "z": 2.7, "d": 1.0, "y": 2.5}
LEAD, BACKLOG = 1, 1.0
TILE_US, UPDATE_US, SEND_US = 3.5, 4.0, 0.02
OTHER = {"x": "z", "z": "x"}


def offset(first, a, b):
    return (a, b) if first == "x" else (b, a)


def transfers(p, first):
    second = OTHER[first]
    moves = {
        (1, p, 1): (first, (0, 0), "all", 1, offset(first, -1, 0)),
        (1, p, -1): (first, (0, 0), "all", -1, offset(first, 1, 0)),
        (2, p, 1): (first, offset(first, -1, 0), "low", 1, offset(first, 2, 0)),
        (2, p, -1): (first, offset(first, 1, 0), "high", -1, offset(first, 2, 0)),
    }
    for a in RING:
        moves[3, p, 1, a] = (second, offset(first, a, 0), "all", 1, offset(first, a, -1))
        moves[3, p, -1, a] = (second, offset(first, a, 0), "all", -1, offset(first, a, 1))
        moves[4, p, 1, a] = (second, offset(first, a, -1), "low", 1, offset(first, a, 2))
        moves[4, p, -1, a] = (second, offset(first, a, 1), "high", -1, offset(first, a, 2))
        for b in RING:
            moves[(5, p, *offset(first, a, b))] = ("d", offset(first, a, b), "all", 0, offset(first, a, b))
    return moves


GROUPS = ((0, -1), (1, 2))


def plan(phases, hidden):
    total = sum(f for f, _ in phases)
    moves, rules, tasks = {}, [], []
    for p, (_, first) in enumerate(phases):
        moves.update(transfers(p, first))
        third = lambda a: [(3, p, 1, a), (3, p, -1, a)]
        follow = lambda a, b: (5, p, *offset(first, a, b))
        rules.append(([(1, p, 1)], [(2, p, 1)] + third(-1) + [follow(-1, 0)]))
        rules.append(([(1, p, -1)], [(2, p, -1)] + third(1) + [follow(1, 0)]))
        rules.append(([(2, p, 1), (2, p, -1)], third(2) + [follow(2, 0)]))
        for a in RING:
            rules.append(([(3, p, 1, a)], [(4, p, 1, a), follow(a, -1)]))
            rules.append(([(3, p, -1, a)], [(4, p, -1, a), follow(a, 1)]))
            rules.append(([(4, p, 1, a), (4, p, -1, a)], [follow(a, 2)]))
        size = phases[p][0]
        needs_all = set()
        for dx in RING:
            for group in GROUPS:
                needs = {n for n, m in moves.items() if n[1] == p and m[4][0] == dx and m[4][1] in group}
                tasks.append((("mm", p, dx, group), needs, TILE_US / 8 * -(-size // 256)))
                needs_all.add(("mm", p, dx, group))
        share = UPDATE_US * size / total
        tasks.append((("update", p), needs_all, share))
        if MODES[p] == "all":
            tasks.append((("reduce", p), {("RS", p)}, share / 8))
        else:
            tasks.append((("halve", p), {("RS", p)}, share / 8))
            tasks.append((("reduce", p), {("PAIR", p)}, share / 16))
            tasks.append((("forward", p), {("AGZ", p)}, 0.02))
        tasks.append((("final", p), {("AG", p)}, 0.02))

    steps, arrivals, free, done, arrived, waited = [], [], {}, set(), set(), set()
    pending = {}
    clock, serial = 0.0, 0

    def urgency(name):
        stage, p = name[:2]
        return p - LEAD * (stage < 3) - 0.25 * (stage in (2, 4)), stage != 3 or name[3] != 2

    def request(names):
        for name in names:
            link, _, _, way, _ = moves[name]
            pending.setdefault((link, way), []).append(name)

    def push(name, lane, took, delay):
        nonlocal serial
        free[lane] = max(clock, free.get(lane, 0.0)) + took
        heapq.heappush(arrivals, (free[lane] + delay, serial, name))
        serial += 1

    def pump():
        nonlocal clock
        sent = []
        for lane, names in pending.items():
            while names and free.get(lane, 0.0) - clock < BACKLOG:
                name = min(names, key=urgency)
                names.remove(name)
                size = phases[name[1]][0] * 512 * (1.0 if moves[name][2] == "all" else 0.5)
                push(name, lane, size / RATE[lane[0]], DELAY[lane[0]])
                clock += SEND_US
                sent.append(name)
        if sent:
            steps.append(("send", tuple(sent)))

    def exchange(kind, p):
        size = phases[p][0] * hidden * 4
        y_part = lambda name, part: push((name, p), "y", size * part / RATE["y"], DELAY["y"] + (MODES[p] == "all"))
        z_part = lambda name, part: push((name, p), ("z", 1), size * part / RATE["x"], DELAY["x"])
        if MODES[p] == "all":
            y_part(kind, 0.75)
        elif MODES[p] == "zy":
            {"RS": z_part, "PAIR": y_part, "AG": y_part, "forward": z_part}[kind](
                {"AG": "AGZ", "forward": "AG"}.get(kind, kind), 0.5 if kind in ("RS", "forward") else 0.375
            )
        elif kind == "AG":
            y_part("AGY", 0.375)
            z_part("AGZ", 0.125)
        elif kind == "PAIR":
            z_part(kind, 0.125)
        else:
            y_part("AG" if kind == "forward" else kind, 0.375 if kind == "forward" else 0.75)

    for p, (_, first) in enumerate(phases):
        request([(1, p, 1), (1, p, -1), (3, p, 1, 0), (3, p, -1, 0), (5, p, 0, 0)])
    pump()
    rank = {"reduce": 0, "halve": 1, "forward": 2, "update": 3, "mm": 4, "final": 5}
    after = {"update": "RS", "halve": "PAIR", "reduce": "AG", "forward": "forward"}
    while rules or tasks:
        while arrivals and arrivals[0][0] <= clock:
            arrived.add(heapq.heappop(arrivals)[2])
        rule = next((r for r in rules if set(r[0]) <= arrived), None)
        if rule:
            rules.remove(rule)
            for name in rule[0]:
                waited.add(name)
                steps.append(("wait", name))
            request(rule[1])
            pump()
            continue
        ready = [t for t in tasks if t[1] <= (arrived | done)]
        if ready:
            task = min(ready, key=lambda t: (rank[t[0][0]], t[0][1]))
            tasks.remove(task)
            for name in sorted(task[1] - waited - done, key=str):
                waited.add(name)
                steps.append(("wait", name))
            steps.append(task[0])
            clock += task[2]
            done.add(task[0])
            if task[0][0] in after:
                exchange(after[task[0][0]], task[0][1])
            pump()
            continue
        clock = arrivals[0][0]
        pump()
    return steps, moves, clock


def make_kernel(phases, features, hidden, tokens, replicas):
    steps, moves, _ = plan(phases, hidden)
    sizes = [f for f, _ in phases]
    starts = [sum(sizes[:p]) for p in range(len(sizes))]
    index = {name: i for i, name in enumerate(sorted(moves, key=str))}
    share = hidden // replicas
    ny = replicas // 2

    def kernel(
        act, grad, w_hbm, m_hbm, v_hbm, an_hbm, mean_hbm,
        held, g_buf, w_buf, m_buf, v_buf, an_buf, acc, landed, mean,
        out_sem, in_sem, rs_out, rs_in, ag_out, ag_in, load_sem, put_sem,
    ):
        me_r, me_t = lax.axis_index("replica"), lax.axis_index("tensor")
        core = lax.rem(me_t, NC)
        zh = lax.rem(me_t // NC, NZ)
        x = me_t // (NC * NZ)
        zl = me_r // ny
        y = lax.rem(me_r, ny)

        def slot(dx, dz, c):
            return (lax.rem(x + dx + NX, NX) * NZ + lax.rem(zh + dz + NZ, NZ)) * NC + c

        def device(dx, dz, c):
            return {"replica": me_r, "tensor": slot(dx, dz, c)}

        def place(j, sign=1):
            there = lax.rem(zl + j // ny, 2)
            return there, lax.rem(y + sign * (j % ny) + ny, ny)

        def replica(j):
            there, row = place(j)
            return {"replica": there * ny + row, "tensor": me_t}

        loads = [
            pltpu.make_async_copy(src, dst, load_sem.at[i])
            for i, (src, dst) in enumerate(
                ((act, held.at[me_t]), (grad, g_buf), (w_hbm, w_buf), (m_hbm, m_buf), (v_hbm, v_buf), (an_hbm, an_buf))
            )
        ]
        for load in loads:
            load.start()

        barrier = pltpu.get_barrier_semaphore()
        friends = [device(0, 1, core), device(0, -1, core), device(1, 0, core), device(-1, 0, core), device(0, 0, 1 - core)]
        friends += [replica(j) for j in range(1, replicas)]
        for friend in friends:
            pl.semaphore_signal(barrier, inc=1, device_id=friend, device_id_type=MESH)
        pl.semaphore_wait(barrier, len(friends))

        def rows_of(name):
            p, part = name[1], moves[name][2]
            half = sizes[p] // 2
            begin = starts[p] + (half if part == "high" else 0)
            return pl.ds(begin, sizes[p] if part == "all" else half)

        def outgoing(name):
            link, source, _, way, _ = moves[name]
            rows = rows_of(name)
            there = slot(*source, core)
            target = {"x": device(way, 0, core), "z": device(0, way, core), "d": device(0, 0, 1 - core)}[link]
            src = act.at[rows] if source == (0, 0) else held.at[there, rows]
            return pltpu.make_async_remote_copy(
                src_ref=src,
                dst_ref=held.at[there, rows],
                send_sem=out_sem.at[index[name]],
                recv_sem=in_sem.at[index[name]],
                device_id=target,
                device_id_type=MESH,
            )

        def incoming(name):
            link, _, _, _, got = moves[name]
            spot = held.at[slot(*got, 1 - core if link == "d" else core), rows_of(name)]
            return pltpu.make_async_remote_copy(
                src_ref=spot,
                dst_ref=spot,
                send_sem=out_sem.at[index[name]],
                recv_sem=in_sem.at[index[name]],
                device_id=device(0, 0, 1 - core),
                device_id_type=MESH,
            )

        def columns(p):
            return pl.ds(starts[p], sizes[p])

        def shares(p, place):
            there, row = place
            return pl.ds(pl.multiple_of((there * ny + row if MODES[p] == "zy" else row * 2 + there) * share, 8), share)

        def both(row):
            return pl.ds(pl.multiple_of(row * 2 * share, 8), 2 * share)

        def half(there):
            return pl.ds(pl.multiple_of(there * ny * share, 8), ny * share)

        def remote(src, dst, out, into, target):
            return pltpu.make_async_remote_copy(
                src_ref=src, dst_ref=dst, send_sem=out, recv_sem=into, device_id=target, device_id_type=MESH
            )

        def landing(at, count=1):
            return pl.ds(at * share, count * share)

        def summand(p, rows, spot, at, j):
            cols = columns(p)
            return remote(acc.at[rows, cols], landed.at[spot, cols], rs_out.at[p, at], rs_in.at[p, at], replica(j))

        def scatter(p):
            if MODES[p] == "all":
                return [summand(p, shares(p, place(j)), landing(j - 1), j - 1, j) for j in range(1, replicas)]
            if MODES[p] == "zy":
                return [summand(p, half(1 - zl), landing(0, ny), 0, ny)]
            return [summand(p, both(place(j)[1]), landing(2 * (j - 1), 2), j - 1, j) for j in range(1, ny)]

        def pair(p):
            if MODES[p] == "all":
                return []
            if MODES[p] == "zy":
                return [summand(p, shares(p, place(j)), landing(ny + j - 1), j, j) for j in range(1, ny)]
            return [summand(p, shares(p, place(ny)), landing(replicas - 2), ny - 1, ny)]

        def result(p, rows, at, j):
            ref = mean.at[rows, columns(p)]
            return remote(ref, ref, ag_out.at[p, at], ag_in.at[p, at], replica(j))

        def spread(p, sent=True, offsets=None):
            last = {"all": replicas, "zy": ny, "yz": ny + 1}[MODES[p]]
            return [
                result(p, shares(p, (zl, y) if sent else place(j, -1)), j - 1, j) for j in offsets or range(1, last)
            ]

        def forward(p, sent=True):
            if MODES[p] == "all":
                return []
            if MODES[p] == "zy":
                return [result(p, half(zl if sent else 1 - zl), ny - 1, ny)]
            return [
                result(p, shares(p, (1 - zl, y) if sent else (1 - zl, place(j, -1)[1])), ny + j - 1, j)
                for j in range(1, ny)
            ]

        def matmul(p, dx, group, first):
            cols = columns(p)

            def product(dz, c):
                block = slot(dx, dz, c)
                left = g_buf[:, pl.ds(pl.multiple_of(block * tokens, tokens), tokens)]
                return lax.dot_general(left, held[block, cols, :], (((1,), (1,)), ((), ())), preferred_element_type=jnp.float32)

            low = min(group)
            if first:
                acc[:, cols] = product(low, 0) + product(low, 1)

            @pl.loop(1 if first else 0, len(group))
            def _(i):
                acc[:, cols] += product(low + i, 0) + product(low + i, 1)

        def update(p):
            cols = columns(p)
            step = 32

            @pl.loop(0, hidden // step)
            def _(i):
                rows = pl.ds(pl.multiple_of(i * step, step), step)
                gradient = acc[rows, cols]
                weights = w_buf[rows, cols]
                moment_one = BETA_ONE * m_buf[rows, cols] + (1.0 - BETA_ONE) * gradient
                moment_two = BETA_TWO * v_buf[rows, cols] + (1.0 - BETA_TWO) * gradient * gradient
                size = moment_one * (1.0 / BIAS_ONE) / (jnp.sqrt(moment_two * (1.0 / BIAS_TWO)) + EPSILON)
                updated = weights - INNER_RATE * (size + DECAY_RATE * weights)
                acc[rows, cols] = an_buf[rows, cols] - updated

        def halve(p):
            cols = columns(p)
            if MODES[p] == "zy":
                for row in range(ny):
                    rows = shares(p, (zl, row))
                    acc[rows, cols] = acc[rows, cols] + landed[landing(row), cols]
            else:
                for there in (1 - zl, zl):
                    rows = shares(p, (there, y))
                    total = acc[rows, cols]
                    for j in range(ny - 1):
                        total = total + landed[pl.ds(pl.multiple_of((j * 2 + there) * share, 8), share), cols]
                    acc[rows, cols] = total

        def reduce(p):
            cols = columns(p)
            rows = shares(p, (zl, y))
            total = acc[rows, cols]
            for at in {"all": range(replicas - 1), "zy": range(ny, replicas - 1), "yz": (replicas - 2,)}[MODES[p]]:
                total = total + landed[landing(at), cols]
            mean[rows, cols] = total * (1.0 / replicas)

        multiplied, loaded = set(), set()

        def load_wait(*which):
            for i in which:
                if i not in loaded:
                    loaded.add(i)
                    loads[i].wait()

        def wait(name):
            kind, p = name[:2]
            copies = {
                "RS": lambda: scatter(p),
                "PAIR": lambda: pair(p),
                "AGZ": lambda: spread(p, False, (ny,) if MODES[p] == "yz" else None),
                "AG": lambda: {
                    "all": lambda: spread(p, False),
                    "zy": lambda: forward(p, False),
                    "yz": lambda: spread(p, False, range(1, ny)) + forward(p, False),
                }[MODES[p]](),
            }.get(kind, lambda: [incoming(name)])
            for copy in copies():
                copy.wait_recv()

        def start(copies):
            for copy in copies:
                copy.start()

        for kind, *rest in steps:
            p = rest[0]
            if kind == "send":
                start(outgoing(name) for name in rest[0])
            elif kind == "forward":
                start(forward(p))
            elif kind == "wait":
                wait(rest[0])
            elif kind == "mm":
                load_wait(0, 1)
                matmul(*rest, p not in multiplied)
                multiplied.add(p)
            elif kind == "update":
                load_wait(2, 3, 4, 5)
                update(p)
                start(scatter(p))
            elif kind == "halve":
                halve(p)
                start(pair(p))
            elif kind == "reduce":
                reduce(p)
                start(spread(p))
            elif kind == "final":
                pltpu.make_async_copy(mean.at[:, columns(p)], mean_hbm.at[:, columns(p)], put_sem.at[p]).start()
        for p in range(len(sizes)):
            pltpu.make_async_copy(mean.at[:, columns(p)], mean_hbm.at[:, columns(p)], put_sem.at[p]).wait()
        for name in index:
            outgoing(name).wait_send()
        for p in range(len(sizes)):
            for copy in [*scatter(p), *pair(p), *spread(p), *forward(p)]:
                copy.wait_send()

    count = len(index)
    full = (hidden, features)
    scratch = [
        pltpu.VMEM((NX * NZ * NC, features, tokens), jnp.bfloat16),
        pltpu.VMEM((hidden, NX * NZ * NC * tokens), jnp.bfloat16),
        *[pltpu.VMEM(full, jnp.float32)] * 4,
        pltpu.VMEM(full, jnp.float32),
        pltpu.VMEM(((replicas - 1) * share, features), jnp.float32),
        pltpu.VMEM(full, jnp.float32),
        pltpu.SemaphoreType.DMA((count,)),
        pltpu.SemaphoreType.DMA((count,)),
        *[pltpu.SemaphoreType.DMA((len(sizes), replicas - 1))] * 4,
        pltpu.SemaphoreType.DMA((6,)),
        pltpu.SemaphoreType.DMA((len(sizes),)),
    ]
    return kernel, scratch


def on_device(activations, out_grad, master_weights, first_moment, second_moment, anchor, outer_momentum):
    tokens, features = activations.shape
    hidden = out_grad.shape[1]
    replicas = lax.axis_size("replica")
    kernel, scratch = make_kernel(PHASES, features, hidden, tokens, replicas)
    operands = (activations, out_grad, master_weights, first_moment, second_moment, anchor)
    pseudo_mean = pl.pallas_call(
        kernel,
        out_shape=jax.ShapeDtypeStruct((hidden, features), jnp.float32),
        in_specs=[pl.BlockSpec(memory_space=pl.ANY)] * 6,
        out_specs=pl.BlockSpec(memory_space=pl.ANY),
        scratch_shapes=scratch,
        compiler_params=pltpu.CompilerParams(collective_id=0, has_side_effects=True, vmem_limit_bytes=60 * 2**20),
        name="diloco",
    )(*(a.T for a in operands)).T
    new_momentum = NESTEROV * outer_momentum + pseudo_mean
    rebuilt = anchor - OUTER_RATE * (pseudo_mean + NESTEROV * new_momentum)
    return rebuilt.astype(jnp.bfloat16), new_momentum


def solution(mesh):
    placed = (
        P(("replica", "tensor"), None),
        P("replica", "tensor"),
        P("replica", "tensor"),
        P("replica", "tensor"),
        P("replica", "tensor"),
        P(None, "tensor"),
        P(None, "tensor"),
    )
    return jax.shard_map(
        on_device,
        mesh=mesh,
        in_specs=placed,
        out_specs=(P(None, "tensor"), P(None, "tensor")),
        check_vma=False,
    )
```

```python
import heapq

import jax
import jax.numpy as jnp
from jax import lax
from jax.experimental import pallas as pl
from jax.experimental.pallas import tpu as pltpu
from jax.sharding import PartitionSpec as P

BETA_ONE = 0.9
BETA_TWO = 0.95
BIAS_ONE = 0.9999734386
BIAS_TWO = 0.9940794708
EPSILON = 1e-08
INNER_RATE = 0.25
DECAY_RATE = 0.1
OUTER_RATE = 0.7
NESTEROV = 0.9

MESH = pl.DeviceIdType.MESH
NX, NZ, NC = 4, 4, 2
RING = (0, -1, 1, 2)

PHASES = ((128, 'z'), (128, 'z'), (128, 'z'), (128, 'z'), (128, 'z'), (128, 'z'), (64, 'z'))
MODES = ('yz', 'yz', 'yz', 'yz', 'yz', 'all', 'all')
RATE = {'x': 47000.0, 'z': 15400.0, 'd': 278000.0, 'y': 62000.0}
DELAY = {'x': 2.75, 'z': 3.98, 'd': 2.2, 'y': 2.78}
LEAD, BACKLOG, RELAY = 0.5, 0.75, -0.3
TILE_US, UPDATE_US, SEND_US = 3.5, 4.0, 0.02
OTHER = {"x": "z", "z": "x"}


def offset(first, a, b):
    return (a, b) if first == "x" else (b, a)


def transfers(p, first):
    second = OTHER[first]
    moves = {
        (1, p, 1): (first, (0, 0), "all", 1, offset(first, -1, 0)),
        (1, p, -1): (first, (0, 0), "all", -1, offset(first, 1, 0)),
        (2, p, 1): (first, offset(first, -1, 0), "low", 1, offset(first, 2, 0)),
        (2, p, -1): (first, offset(first, 1, 0), "high", -1, offset(first, 2, 0)),
    }
    for a in RING:
        moves[3, p, 1, a] = (second, offset(first, a, 0), "all", 1, offset(first, a, -1))
        moves[3, p, -1, a] = (second, offset(first, a, 0), "all", -1, offset(first, a, 1))
        moves[4, p, 1, a] = (second, offset(first, a, -1), "low", 1, offset(first, a, 2))
        moves[4, p, -1, a] = (second, offset(first, a, 1), "high", -1, offset(first, a, 2))
        for b in RING:
            moves[(5, p, *offset(first, a, b))] = ("d", offset(first, a, b), "all", 0, offset(first, a, b))
    return moves


GROUPS = ((0, -1), (1, 2))


def plan(phases, hidden):
    total = sum(f for f, _ in phases)
    moves, rules, tasks = {}, [], []
    for p, (_, first) in enumerate(phases):
        moves.update(transfers(p, first))
        third = lambda a: [(3, p, 1, a), (3, p, -1, a)]
        follow = lambda a, b: (5, p, *offset(first, a, b))
        rules.append(([(1, p, 1)], [(2, p, 1)] + third(-1) + [follow(-1, 0)]))
        rules.append(([(1, p, -1)], [(2, p, -1)] + third(1) + [follow(1, 0)]))
        rules.append(([(2, p, 1), (2, p, -1)], third(2) + [follow(2, 0)]))
        for a in RING:
            rules.append(([(3, p, 1, a)], [(4, p, 1, a), follow(a, -1)]))
            rules.append(([(3, p, -1, a)], [(4, p, -1, a), follow(a, 1)]))
            rules.append(([(4, p, 1, a), (4, p, -1, a)], [follow(a, 2)]))
        size = phases[p][0]
        needs_all = set()
        for dx in RING:
            for group in GROUPS:
                needs = {n for n, m in moves.items() if n[1] == p and m[4][0] == dx and m[4][1] in group}
                tasks.append((("mm", p, dx, group), needs, TILE_US / 8 * -(-size // 256)))
                needs_all.add(("mm", p, dx, group))
        share = UPDATE_US * size / total
        tasks.append((("update", p), needs_all, share))
        if MODES[p] == "all":
            tasks.append((("reduce", p), {("RS", p)}, share / 8))
        else:
            tasks.append((("halve", p), {("RS", p)}, share / 8))
            tasks.append((("reduce", p), {("PAIR", p)}, share / 16))
            tasks.append((("forward", p), {("AGZ", p)}, 0.02))
        tasks.append((("final", p), {("AG", p)}, 0.02))

    steps, arrivals, free, done, arrived, waited = [], [], {}, set(), set(), set()
    pending = {}
    clock, serial = 0.0, 0

    def urgency(name):
        stage, p = name[:2]
        return p - LEAD * (stage < 3) - RELAY * (stage in (2, 4)), stage != 3 or name[3] != 2

    def request(names):
        for name in names:
            link, _, _, way, _ = moves[name]
            pending.setdefault((link, way), []).append(name)

    def push(name, lane, took, delay):
        nonlocal serial
        free[lane] = max(clock, free.get(lane, 0.0)) + took
        heapq.heappush(arrivals, (free[lane] + delay, serial, name))
        serial += 1

    def pump():
        nonlocal clock
        sent = []
        for lane, names in pending.items():
            while names and free.get(lane, 0.0) - clock < BACKLOG:
                name = min(names, key=urgency)
                names.remove(name)
                size = phases[name[1]][0] * 512 * (1.0 if moves[name][2] == "all" else 0.5)
                push(name, lane, size / RATE[lane[0]], DELAY[lane[0]])
                clock += SEND_US
                sent.append(name)
        if sent:
            steps.append(("send", tuple(sent)))

    def exchange(kind, p):
        size = phases[p][0] * hidden * 4
        y_part = lambda name, part: push((name, p), "y", size * part / RATE["y"], DELAY["y"] + (MODES[p] == "all"))
        z_part = lambda name, part: push((name, p), ("z", 1), size * part / RATE["x"], DELAY["x"])
        if MODES[p] == "all":
            y_part(kind, 0.75)
        elif MODES[p] == "zy":
            {"RS": z_part, "PAIR": y_part, "AG": y_part, "forward": z_part}[kind](
                {"AG": "AGZ", "forward": "AG"}.get(kind, kind), 0.5 if kind in ("RS", "forward") else 0.375
            )
        elif kind == "AG":
            y_part("AGY", 0.375)
            z_part("AGZ", 0.125)
        elif kind == "PAIR":
            z_part(kind, 0.125)
        else:
            y_part("AG" if kind == "forward" else kind, 0.375 if kind == "forward" else 0.75)

    for p, (_, first) in enumerate(phases):
        request([(1, p, 1), (1, p, -1), (3, p, 1, 0), (3, p, -1, 0), (5, p, 0, 0)])
    pump()
    rank = {"reduce": 0, "halve": 1, "forward": 2, "update": 3, "mm": 4, "final": 5}
    after = {"update": "RS", "halve": "PAIR", "reduce": "AG", "forward": "forward"}
    while rules or tasks:
        while arrivals and arrivals[0][0] <= clock:
            arrived.add(heapq.heappop(arrivals)[2])
        rule = next((r for r in rules if set(r[0]) <= arrived), None)
        if rule:
            rules.remove(rule)
            for name in rule[0]:
                waited.add(name)
                steps.append(("wait", name))
            request(rule[1])
            pump()
            continue
        ready = [t for t in tasks if t[1] <= (arrived | done)]
        if ready:
            task = min(ready, key=lambda t: (rank[t[0][0]], t[0][1]))
            tasks.remove(task)
            for name in sorted(task[1] - waited - done, key=str):
                waited.add(name)
                steps.append(("wait", name))
            steps.append(task[0])
            clock += task[2]
            done.add(task[0])
            if task[0][0] in after:
                exchange(after[task[0][0]], task[0][1])
            pump()
            continue
        clock = arrivals[0][0]
        pump()
    return steps, moves, clock


def make_kernel(phases, features, hidden, tokens, replicas):
    steps, moves, _ = plan(phases, hidden)
    sizes = [f for f, _ in phases]
    starts = [sum(sizes[:p]) for p in range(len(sizes))]
    index = {name: i for i, name in enumerate(sorted(moves, key=str))}
    share = hidden // replicas
    ny = replicas // 2

    def kernel(
        act, grad, w_hbm, m_hbm, v_hbm, an_hbm, mean_hbm,
        held, g_buf, w_buf, m_buf, v_buf, an_buf, acc, landed, mean,
        out_sem, in_sem, rs_out, rs_in, ag_out, ag_in, load_sem, put_sem,
    ):
        me_r, me_t = lax.axis_index("replica"), lax.axis_index("tensor")
        core = lax.rem(me_t, NC)
        zh = lax.rem(me_t // NC, NZ)
        x = me_t // (NC * NZ)
        zl = me_r // ny
        y = lax.rem(me_r, ny)

        def slot(dx, dz, c):
            return (lax.rem(x + dx + NX, NX) * NZ + lax.rem(zh + dz + NZ, NZ)) * NC + c

        def device(dx, dz, c):
            return {"replica": me_r, "tensor": slot(dx, dz, c)}

        def place(j, sign=1):
            there = lax.rem(zl + j // ny, 2)
            return there, lax.rem(y + sign * (j % ny) + ny, ny)

        def replica(j):
            there, row = place(j)
            return {"replica": there * ny + row, "tensor": me_t}

        loads = [
            pltpu.make_async_copy(src, dst, load_sem.at[i])
            for i, (src, dst) in enumerate(
                ((act, held.at[me_t]), (grad, g_buf), (w_hbm, w_buf), (m_hbm, m_buf), (v_hbm, v_buf), (an_hbm, an_buf))
            )
        ]
        for load in loads:
            load.start()

        barrier = pltpu.get_barrier_semaphore()
        friends = [device(0, 1, core), device(0, -1, core), device(1, 0, core), device(-1, 0, core), device(0, 0, 1 - core)]
        friends += [replica(j) for j in range(1, replicas)]
        for friend in friends:
            pl.semaphore_signal(barrier, inc=1, device_id=friend, device_id_type=MESH)
        pl.semaphore_wait(barrier, len(friends))

        def rows_of(name):
            p, part = name[1], moves[name][2]
            half = sizes[p] // 2
            begin = starts[p] + (half if part == "high" else 0)
            return pl.ds(begin, sizes[p] if part == "all" else half)

        def outgoing(name):
            link, source, _, way, _ = moves[name]
            rows = rows_of(name)
            there = slot(*source, core)
            target = {"x": device(way, 0, core), "z": device(0, way, core), "d": device(0, 0, 1 - core)}[link]
            src = act.at[rows] if source == (0, 0) else held.at[there, rows]
            return pltpu.make_async_remote_copy(
                src_ref=src,
                dst_ref=held.at[there, rows],
                send_sem=out_sem.at[index[name]],
                recv_sem=in_sem.at[index[name]],
                device_id=target,
                device_id_type=MESH,
            )

        def incoming(name):
            link, _, _, _, got = moves[name]
            spot = held.at[slot(*got, 1 - core if link == "d" else core), rows_of(name)]
            return pltpu.make_async_remote_copy(
                src_ref=spot,
                dst_ref=spot,
                send_sem=out_sem.at[index[name]],
                recv_sem=in_sem.at[index[name]],
                device_id=device(0, 0, 1 - core),
                device_id_type=MESH,
            )

        def columns(p):
            return pl.ds(starts[p], sizes[p])

        def shares(p, place):
            there, row = place
            return pl.ds(pl.multiple_of((there * ny + row if MODES[p] == "zy" else row * 2 + there) * share, 8), share)

        def both(row):
            return pl.ds(pl.multiple_of(row * 2 * share, 8), 2 * share)

        def half(there):
            return pl.ds(pl.multiple_of(there * ny * share, 8), ny * share)

        def remote(src, dst, out, into, target):
            return pltpu.make_async_remote_copy(
                src_ref=src, dst_ref=dst, send_sem=out, recv_sem=into, device_id=target, device_id_type=MESH
            )

        def landing(at, count=1):
            return pl.ds(at * share, count * share)

        def summand(p, rows, spot, at, j):
            cols = columns(p)
            return remote(acc.at[rows, cols], landed.at[spot, cols], rs_out.at[p, at], rs_in.at[p, at], replica(j))

        def scatter(p):
            if MODES[p] == "all":
                return [summand(p, shares(p, place(j)), landing(j - 1), j - 1, j) for j in range(1, replicas)]
            if MODES[p] == "zy":
                return [summand(p, half(1 - zl), landing(0, ny), 0, ny)]
            return [summand(p, both(place(j)[1]), landing(2 * (j - 1), 2), j - 1, j) for j in range(1, ny)]

        def pair(p):
            if MODES[p] == "all":
                return []
            if MODES[p] == "zy":
                return [summand(p, shares(p, place(j)), landing(ny + j - 1), j, j) for j in range(1, ny)]
            return [summand(p, shares(p, place(ny)), landing(replicas - 2), ny - 1, ny)]

        def result(p, rows, at, j):
            ref = mean.at[rows, columns(p)]
            return remote(ref, ref, ag_out.at[p, at], ag_in.at[p, at], replica(j))

        def spread(p, sent=True, offsets=None):
            last = {"all": replicas, "zy": ny, "yz": ny + 1}[MODES[p]]
            return [
                result(p, shares(p, (zl, y) if sent else place(j, -1)), j - 1, j) for j in offsets or range(1, last)
            ]

        def forward(p, sent=True):
            if MODES[p] == "all":
                return []
            if MODES[p] == "zy":
                return [result(p, half(zl if sent else 1 - zl), ny - 1, ny)]
            return [
                result(p, shares(p, (1 - zl, y) if sent else (1 - zl, place(j, -1)[1])), ny + j - 1, j)
                for j in range(1, ny)
            ]

        def matmul(p, dx, group, first):
            cols = columns(p)

            def product(dz, c):
                block = slot(dx, dz, c)
                left = g_buf[:, pl.ds(pl.multiple_of(block * tokens, tokens), tokens)]
                return lax.dot_general(left, held[block, cols, :], (((1,), (1,)), ((), ())), preferred_element_type=jnp.float32)

            low = min(group)
            if first:
                acc[:, cols] = product(low, 0) + product(low, 1)

            @pl.loop(1 if first else 0, len(group))
            def _(i):
                acc[:, cols] += product(low + i, 0) + product(low + i, 1)

        def update(p):
            cols = columns(p)
            step = 32

            @pl.loop(0, hidden // step)
            def _(i):
                rows = pl.ds(pl.multiple_of(i * step, step), step)
                gradient = acc[rows, cols]
                weights = w_buf[rows, cols]
                moment_one = BETA_ONE * m_buf[rows, cols] + (1.0 - BETA_ONE) * gradient
                moment_two = BETA_TWO * v_buf[rows, cols] + (1.0 - BETA_TWO) * gradient * gradient
                size = moment_one * (1.0 / BIAS_ONE) / (jnp.sqrt(moment_two * (1.0 / BIAS_TWO)) + EPSILON)
                updated = weights - INNER_RATE * (size + DECAY_RATE * weights)
                acc[rows, cols] = an_buf[rows, cols] - updated

        def halve(p):
            cols = columns(p)
            if MODES[p] == "zy":
                for row in range(ny):
                    rows = shares(p, (zl, row))
                    acc[rows, cols] = acc[rows, cols] + landed[landing(row), cols]
            else:
                for there in (1 - zl, zl):
                    rows = shares(p, (there, y))
                    total = acc[rows, cols]
                    for j in range(ny - 1):
                        total = total + landed[pl.ds(pl.multiple_of((j * 2 + there) * share, 8), share), cols]
                    acc[rows, cols] = total

        def reduce(p):
            cols = columns(p)
            rows = shares(p, (zl, y))
            total = acc[rows, cols]
            for at in {"all": range(replicas - 1), "zy": range(ny, replicas - 1), "yz": (replicas - 2,)}[MODES[p]]:
                total = total + landed[landing(at), cols]
            mean[rows, cols] = total * (1.0 / replicas)

        multiplied, loaded = set(), set()

        def load_wait(*which):
            for i in which:
                if i not in loaded:
                    loaded.add(i)
                    loads[i].wait()

        def wait(name):
            kind, p = name[:2]
            copies = {
                "RS": lambda: scatter(p),
                "PAIR": lambda: pair(p),
                "AGZ": lambda: spread(p, False, (ny,) if MODES[p] == "yz" else None),
                "AG": lambda: {
                    "all": lambda: spread(p, False),
                    "zy": lambda: forward(p, False),
                    "yz": lambda: spread(p, False, range(1, ny)) + forward(p, False),
                }[MODES[p]](),
            }.get(kind, lambda: [incoming(name)])
            for copy in copies():
                copy.wait_recv()

        def start(copies):
            for copy in copies:
                copy.start()

        for kind, *rest in steps:
            p = rest[0]
            if kind == "send":
                start(outgoing(name) for name in rest[0])
            elif kind == "forward":
                start(forward(p))
            elif kind == "wait":
                wait(rest[0])
            elif kind == "mm":
                load_wait(0, 1)
                matmul(*rest, p not in multiplied)
                multiplied.add(p)
            elif kind == "update":
                load_wait(2, 3, 4, 5)
                update(p)
                start(scatter(p))
            elif kind == "halve":
                halve(p)
                start(pair(p))
            elif kind == "reduce":
                reduce(p)
                start(spread(p))
            elif kind == "final":
                pltpu.make_async_copy(mean.at[:, columns(p)], mean_hbm.at[:, columns(p)], put_sem.at[p]).start()
        for p in range(len(sizes)):
            pltpu.make_async_copy(mean.at[:, columns(p)], mean_hbm.at[:, columns(p)], put_sem.at[p]).wait()
        for name in index:
            outgoing(name).wait_send()
        for p in range(len(sizes)):
            for copy in [*scatter(p), *pair(p), *spread(p), *forward(p)]:
                copy.wait_send()

    count = len(index)
    full = (hidden, features)
    scratch = [
        pltpu.VMEM((NX * NZ * NC, features, tokens), jnp.bfloat16),
        pltpu.VMEM((hidden, NX * NZ * NC * tokens), jnp.bfloat16),
        *[pltpu.VMEM(full, jnp.float32)] * 4,
        pltpu.VMEM(full, jnp.float32),
        pltpu.VMEM(((replicas - 1) * share, features), jnp.float32),
        pltpu.VMEM(full, jnp.float32),
        pltpu.SemaphoreType.DMA((count,)),
        pltpu.SemaphoreType.DMA((count,)),
        *[pltpu.SemaphoreType.DMA((len(sizes), replicas - 1))] * 4,
        pltpu.SemaphoreType.DMA((6,)),
        pltpu.SemaphoreType.DMA((len(sizes),)),
    ]
    return kernel, scratch


def on_device(activations, out_grad, master_weights, first_moment, second_moment, anchor, outer_momentum):
    tokens, features = activations.shape
    hidden = out_grad.shape[1]
    replicas = lax.axis_size("replica")
    kernel, scratch = make_kernel(PHASES, features, hidden, tokens, replicas)
    operands = (activations, out_grad, master_weights, first_moment, second_moment, anchor)
    pseudo_mean = pl.pallas_call(
        kernel,
        out_shape=jax.ShapeDtypeStruct((hidden, features), jnp.float32),
        in_specs=[pl.BlockSpec(memory_space=pl.ANY)] * 6,
        out_specs=pl.BlockSpec(memory_space=pl.ANY),
        scratch_shapes=scratch,
        compiler_params=pltpu.CompilerParams(collective_id=0, has_side_effects=True, vmem_limit_bytes=60 * 2**20),
        name="diloco",
    )(*(a.T for a in operands)).T
    new_momentum = NESTEROV * outer_momentum + pseudo_mean
    rebuilt = anchor - OUTER_RATE * (pseudo_mean + NESTEROV * new_momentum)
    return rebuilt.astype(jnp.bfloat16), new_momentum


def solution(mesh):
    placed = (
        P(("replica", "tensor"), None),
        P("replica", "tensor"),
        P("replica", "tensor"),
        P("replica", "tensor"),
        P("replica", "tensor"),
        P(None, "tensor"),
        P(None, "tensor"),
    )
    return jax.shard_map(
        on_device,
        mesh=mesh,
        in_specs=placed,
        out_specs=(P(None, "tensor"), P(None, "tensor")),
        check_vma=False,
    )
```
